32 devices in a mesh: grp: 2 (over x), tm: 16 (over z, y, core).
Axes of the slice: x: 2, y: 2, z: 4, core: 2. Of those that a mesh axis runs over, the one named last changes fastest.
Arguments:
- upsampled: bfloat16 [2, 12288, 512], P(None, ('grp', 'tm')), parts along dimension 1, may hold values from -6 to 6
- taps: bfloat16 [3, 7, 512, 512], replicated, may hold values from -0.09375 to 0.09375
- bias_wide: float32 [3, 512], replicated, may hold values from -1.8 to 1.8
- pointwise: bfloat16 [3, 512, 512], replicated, may hold values from -0.25 to 0.25
- bias_point: float32 [3, 512], replicated, may hold values from -1.8 to 1.8
- alpha_in: float32 [3, 512], replicated, may hold values from 0.5 to 4
- beta_in: float32 [3, 512], replicated, may hold values from 0.5 to 4
- alpha_mid: float32 [3, 512], replicated, may hold values from 0.5 to 4
- beta_mid: float32 [3, 512], replicated, may hold values from 0.5 to 4
Outputs:
- decoded: bfloat16 [12288, 512], P(('grp', 'tm')), parts along dimension 0
The draws below stay inside these ranges and needn't reach their ends.
There are 2 independent parts, one for each index of `grp`. The reference program is written for one: setup_inputs(seed, part) draws one part's arguments, and reference() takes and returns one part's arrays. A program takes and returns all parts, laid end to end along the dimension named above; an argument that names none is the same for every part. Nothing has to cross between parts.
All inputs are finite; a program needn't handle non-finite values.
Results may differ from the reference program's by a relative error of at most 0.027.
The reference program's roundings to bfloat16 on the way count: a program that leaves them out, or rounds other values in their place, can miss the bound.
Values may be sent and summed in bfloat16 or wider, within the bound.
A program may use at most 128 MiB of HBM per device.

```python
import math
import jax
import jax.numpy as jnp

C = 512
KERNEL = 7
STRIDE = 8
UNITS = 3
FRAMES = 6144


def block_levels(stream_key, dims, shards, smallest, high):
    def one(position, parts):
        draws = jax.random.uniform(jax.random.fold_in(jax.random.fold_in(stream_key, 6), position), (parts,), jnp.float32, smallest / len(shards), high / len(shards))
        return jnp.repeat(jnp.exp(draws), dims[position] // parts).reshape((-1,) + (1,) * (len(dims) - position - 1))

    gain = one(*shards[0])
    for cut in shards[1:]:
        gain = gain * one(*cut)
    return gain


def noise(own_key, extent, deviation, most, shards=(), kind=jnp.bfloat16):
    loudness = block_levels(own_key, extent, shards, -0.22, 0.18) if shards else 1.0
    array = jax.random.normal(own_key, extent, jnp.float32) * deviation * loudness
    return jnp.minimum(jnp.maximum(array, -most), most).astype(kind)


def setup_inputs(seed: int = 0, part: int = 0) -> dict:
    key_list = jax.random.split(jax.random.key(seed), 10)
    part_keys = jax.random.split(jax.random.fold_in(key_list[9], part), 10)
    return {
        "upsampled": noise(part_keys[0], (2, FRAMES, C), 1.0, 6.0, ((1, 16),)),
        "taps": noise(key_list[1], (UNITS, KERNEL, C, C), (KERNEL * C) ** -0.5, 0.09375),
        "bias_wide": noise(key_list[2], (UNITS, C), 0.3, 1.8, (), jnp.float32),
        "pointwise": noise(key_list[3], (UNITS, C, C), C ** -0.5, 0.25),
        "bias_point": noise(key_list[4], (UNITS, C), 0.3, 1.8, (), jnp.float32),
        "alpha_in": jnp.clip(jnp.exp(jax.random.uniform(key_list[5], (UNITS, C), jnp.float32, math.log(0.5), math.log(4.0))), 0.5, 4.0),
        "beta_in": jnp.clip(jnp.exp(jax.random.uniform(key_list[6], (UNITS, C), jnp.float32, math.log(0.5), math.log(4.0))), 0.5, 4.0),
        "alpha_mid": jnp.clip(jnp.exp(jax.random.uniform(key_list[7], (UNITS, C), jnp.float32, math.log(0.5), math.log(4.0))), 0.5, 4.0),
        "beta_mid": jnp.clip(jnp.exp(jax.random.uniform(key_list[8], (UNITS, C), jnp.float32, math.log(0.5), math.log(4.0))), 0.5, 4.0),
    }


def snake(values, alpha, beta):
    return values + jnp.square(jnp.sin(alpha * values)) / beta


def residual_unit(inputs, dilation, taps, bias_wide, pointwise, bias_point, alpha_in, beta_in, alpha_mid, beta_mid):
    length = inputs.shape[0] - 6 * dilation
    widened = snake(inputs.astype(jnp.float32), alpha_in, beta_in).astype(jnp.bfloat16)
    middle = jnp.zeros((length, taps.shape[2]), jnp.float32) + bias_wide
    for k in range(KERNEL):
        middle = middle + jnp.dot(widened[k * dilation:k * dilation + length], taps[k], preferred_element_type=jnp.float32)
    gated = snake(middle, alpha_mid, beta_mid).astype(jnp.bfloat16)
    update = jnp.dot(gated, pointwise, preferred_element_type=jnp.float32) + bias_point
    kept = inputs[3 * dilation:3 * dilation + length].astype(jnp.float32)
    return (kept + update).astype(jnp.bfloat16)


def reference(upsampled, taps, bias_wide, pointwise, bias_point, alpha_in, beta_in, alpha_mid, beta_mid):
    frames = upsampled.shape[1]
    shifted = jnp.concatenate([jnp.zeros((STRIDE, upsampled.shape[2]), upsampled.dtype), upsampled[1, :frames - STRIDE]], axis=0)
    current = (upsampled[0].astype(jnp.float32) + shifted.astype(jnp.float32)).astype(jnp.bfloat16)
    dilations = (1, 3, 9)
    for index in range(UNITS):
        spread = 3 * dilations[index]
        padded = jnp.pad(current, ((spread, spread), (0, 0)))
        current = residual_unit(padded, dilations[index], taps[index], bias_wide[index], pointwise[index], bias_point[index], alpha_in[index], beta_in[index], alpha_mid[index], beta_mid[index])
    return current
```

```python
import functools
import math

import jax
import jax.numpy as jnp
from jax import lax
from jax.experimental import pallas as pl
from jax.experimental.pallas import tpu as pltpu
from jax.sharding import PartitionSpec as P

MESH = pl.DeviceIdType.MESH
KERNEL = 7
STRIDE = 8
UNITS = 3
DILATIONS = (1, 3, 9)
LANES = 128
EDGE = 48
MARGIN = (40, 32, 0)
WIDER = (48, 32, 0)
CORE = 160
FIRST_TAPS = ((0, 4), (4, 7))
SQUARE = (9.869524955749512, -32.46514129638672, 42.64342498779297, -29.426273345947266, 10.581298828125)


def snake(values, frequency, inverse):
    turns = values * frequency
    rest = turns - jnp.round(turns)
    square = rest * rest
    poly = SQUARE[-1]
    for coefficient in SQUARE[-2::-1]:
        poly = poly * square + coefficient
    return values + (poly * square) * inverse


def kernel(
    count, frames,
    up_hbm, taps_hbm, bias_wide_hbm, point_hbm, bias_point_hbm,
    alpha_in_hbm, beta_in_hbm, alpha_mid_hbm, beta_mid_hbm,
    out_ref,
    taps_ref, point_ref, ext_ref, x_ref, s_refs,
    bias_wide, bias_point, alpha_in, beta_in, alpha_mid, beta_mid,
    taps_sems, point_sems, small_sems, up_sem, send_sems, recv_sems,
):
    channels = ext_ref.shape[2]
    groups = channels // LANES
    below, above = EDGE, EDGE + frames
    extended = frames + 2 * EDGE
    me = lax.axis_index("tm")
    has_left = me > 0
    has_right = me < count - 1
    barrier = pltpu.get_barrier_semaphore()

    @pl.when(has_left)
    def _():
        pl.semaphore_signal(barrier, inc=1, device_id={"tm": me - 1}, device_id_type=MESH)

    @pl.when(has_right)
    def _():
        pl.semaphore_signal(barrier, inc=1, device_id={"tm": me + 1}, device_id_type=MESH)

    own = pltpu.make_async_copy(up_hbm, ext_ref.at[:, pl.ds(below, frames), :], up_sem)
    own.start()
    smalls = [
        pltpu.make_async_copy(source, target, small_sems.at[i])
        for i, (source, target) in enumerate((
            (alpha_in_hbm, alpha_in), (beta_in_hbm, beta_in), (bias_wide_hbm, bias_wide),
            (alpha_mid_hbm, alpha_mid), (beta_mid_hbm, beta_mid), (bias_point_hbm, bias_point),
        ))
    ]
    for copy in smalls:
        copy.start()

    def tap_copy(unit, k):
        span = pl.ds(k * channels, channels)
        return pltpu.make_async_copy(
            taps_hbm.at[unit, span, :], taps_ref.at[unit, span, :], taps_sems.at[unit, k]
        )

    tap_copies = [[tap_copy(unit, k) for k in range(KERNEL)] for unit in range(UNITS)]
    point_copies = [
        pltpu.make_async_copy(point_hbm.at[unit], point_ref.at[unit], point_sems.at[unit])
        for unit in range(UNITS)
    ]
    for copy in tap_copies[0]:
        copy.start()
    point_copies[0].start()

    @pl.when(has_left & has_right)
    def _():
        pl.semaphore_wait(barrier, 2)

    @pl.when(has_left != has_right)
    def _():
        pl.semaphore_wait(barrier, 1)

    to_right = pltpu.make_async_remote_copy(
        src_ref=up_hbm.at[:, pl.ds(frames - EDGE, EDGE), :],
        dst_ref=ext_ref.at[:, pl.ds(0, EDGE), :],
        send_sem=send_sems.at[0], recv_sem=recv_sems.at[0],
        device_id={"tm": me + 1}, device_id_type=MESH,
    )
    to_left = pltpu.make_async_remote_copy(
        src_ref=up_hbm.at[:, pl.ds(0, EDGE), :],
        dst_ref=ext_ref.at[:, pl.ds(above, EDGE), :],
        send_sem=send_sems.at[1], recv_sem=recv_sems.at[1],
        device_id={"tm": me - 1}, device_id_type=MESH,
    )

    @pl.when(has_right)
    def _():
        to_right.start()

    @pl.when(has_left)
    def _():
        to_left.start()

    for unit in range(1, UNITS):
        for copy in tap_copies[unit]:
            copy.start()
        point_copies[unit].start()

    @pl.when(jnp.logical_not(has_left))
    def _():
        ext_ref[:, 0:EDGE, :] = jnp.zeros((2, EDGE, channels), jnp.bfloat16)

    @pl.when(jnp.logical_not(has_right))
    def _():
        ext_ref[:, above:extended, :] = jnp.zeros((2, EDGE, channels), jnp.bfloat16)

    def row_of(ref, unit):
        return ref[unit : unit + 1, :]

    def blocks(low, high):
        edges = [low, *range(low - low % 16 + 16, high, 16), high]
        return zip(edges[:-1], edges[1:])

    def hold(unit, low, high, values):
        s = snake(values, row_of(alpha_in, unit) * (1.0 / math.pi), 1.0 / row_of(beta_in, unit))
        if high <= below:
            s = jnp.where(has_left, s, 0.0)
        elif low >= above:
            s = jnp.where(has_right, s, 0.0)
        for c in range(groups):
            part = slice(c * LANES, (c + 1) * LANES)
            x_ref[c, low:high, :] = values[:, part]
            s_refs[unit, c, low:high, :] = s[:, part]

    def enter(low, high):
        for start, stop in blocks(low, high):
            whole = start - start % 16
            early = ext_ref[0, whole : whole + 16, :].astype(jnp.float32)
            if whole:
                late = ext_ref[1, whole - 16 : whole + 16, :].astype(jnp.float32)[8:24]
            else:
                late = ext_ref[1, 0:16, :].astype(jnp.float32)
                late = jnp.concatenate([late[0:8], late[0:8]], axis=0)
            x = (early + late)[start - whole : stop - whole]
            hold(0, start, stop, x.astype(jnp.bfloat16).astype(jnp.float32))

    def shifted(unit, pieces, first, last):
        columns = []
        for k in range(first, last):
            offset = (k - KERNEL // 2) * DILATIONS[unit]
            rows = [
                jnp.concatenate(
                    [s_refs[unit, c, low + offset : high + offset, :] for c in range(groups)], axis=1
                )
                for low, high in pieces
            ]
            columns.append(jnp.concatenate(rows, axis=0).astype(jnp.bfloat16))
        return jnp.concatenate(columns, axis=1)

    def wide(unit, pieces, first=0, last=KERNEL):
        weights = taps_ref[unit, first * channels : last * channels, :]
        return jnp.dot(shifted(unit, pieces, first, last), weights, preferred_element_type=jnp.float32)

    def close(unit, pieces, h):
        h = h + row_of(bias_wide, unit)
        g = snake(h, row_of(alpha_mid, unit) * (1.0 / math.pi), 1.0 / row_of(beta_mid, unit))
        update = jnp.dot(g.astype(jnp.bfloat16), point_ref[unit], preferred_element_type=jnp.float32)
        update = update + row_of(bias_point, unit)
        base = 0
        for low, high in pieces:
            for start, stop in blocks(low, high):
                kept = jnp.concatenate([x_ref[c, start:stop, :] for c in range(groups)], axis=1)
                at = base + start - low
                x = (kept + update[at : at + stop - start]).astype(jnp.bfloat16)
                if unit + 1 < UNITS:
                    hold(unit + 1, start, stop, x.astype(jnp.float32))
                else:
                    out_ref[start - below : stop - below, :] = x
            base += high - low

    middle = extended // 2
    cores, rims = [], []
    for unit in range(UNITS):
        low, high = middle - CORE // 2 - WIDER[unit], middle + CORE // 2 + WIDER[unit]
        cores.append(((low, high),))
        rims.append(((below - MARGIN[unit], low), (high, above + MARGIN[unit])))
    inside = (cores[0][0][0] - 16, cores[0][0][1] + 16)

    for copy in smalls:
        copy.wait()
    own.wait()
    enter(*inside)
    core = None
    for first, last in FIRST_TAPS:
        for copy in tap_copies[0][first:last]:
            copy.wait()
        if last == KERNEL:
            point_copies[0].wait()

            @pl.when(has_left)
            def _():
                to_right.wait_recv()

            @pl.when(has_right)
            def _():
                to_left.wait_recv()

        part = wide(0, cores[0], first, last)
        core = part if core is None else core + part
    enter(below - MARGIN[0], inside[0])
    enter(inside[1], above + MARGIN[0])
    rim = None
    for unit in range(UNITS):
        if unit:
            for copy in tap_copies[unit]:
                copy.wait()
            point_copies[unit].wait()
            core = wide(unit, cores[unit])
            close(unit - 1, rims[unit - 1], rim)
        rim = wide(unit, rims[unit])
        close(unit, cores[unit], core)
    close(UNITS - 1, rims[UNITS - 1], rim)

    @pl.when(has_right)
    def _():
        to_right.wait_send()

    @pl.when(has_left)
    def _():
        to_left.wait_send()


def land(held_ref, out_hbm, sem):
    copy = pltpu.make_async_copy(held_ref, out_hbm, sem)
    copy.start()
    copy.wait()


def per_device(
    upsampled, taps, bias_wide, pointwise, bias_point, alpha_in, beta_in, alpha_mid, beta_mid
):
    count = lax.axis_size("tm")
    frames, channels = upsampled.shape[1:]
    extended = frames + 2 * EDGE
    hbm = pl.BlockSpec(memory_space=pltpu.HBM)
    return pl.pallas_call(
        functools.partial(kernel, count, frames),
        out_shape=jax.ShapeDtypeStruct((frames, channels), jnp.bfloat16),
        in_specs=[hbm] * 9,
        out_specs=pl.BlockSpec(memory_space=pltpu.VMEM),
        scratch_shapes=[
            pltpu.VMEM((UNITS, KERNEL * channels, channels), jnp.bfloat16),
            pltpu.VMEM((UNITS, channels, channels), jnp.bfloat16),
            pltpu.VMEM((2, extended, channels), jnp.bfloat16),
            pltpu.VMEM((channels // LANES, extended, LANES), jnp.float32),
            pltpu.VMEM((UNITS, channels // LANES, extended, LANES), jnp.float32),
        ]
        + [pltpu.VMEM((UNITS, channels), jnp.float32)] * 6
        + [
            pltpu.SemaphoreType.DMA((UNITS, KERNEL)),
            pltpu.SemaphoreType.DMA((UNITS,)),
            pltpu.SemaphoreType.DMA((6,)),
            pltpu.SemaphoreType.DMA,
            pltpu.SemaphoreType.DMA((2,)),
            pltpu.SemaphoreType.DMA((2,)),
        ],
        compiler_params=pltpu.CompilerParams(
            vmem_limit_bytes=48 << 20, collective_id=0, has_side_effects=True
        ),
    )(
        upsampled, taps.reshape(UNITS, KERNEL * channels, channels), bias_wide, pointwise,
        bias_point, alpha_in, beta_in, alpha_mid, beta_mid,
    )


def solution(mesh):
    placed = (P(None, ("grp", "tm"), None), P(), P(), P(), P(), P(), P(), P(), P())
    return jax.shard_map(
        per_device, mesh=mesh, in_specs=placed, out_specs=P(("grp", "tm"), None), check_vma=False
    )
```

```python
import functools
import math

import jax
import jax.numpy as jnp
from jax import lax
from jax.experimental import pallas as pl
from jax.experimental.pallas import tpu as pltpu
from jax.sharding import PartitionSpec as P

MESH = pl.DeviceIdType.MESH
KERNEL = 7
STRIDE = 8
UNITS = 3
DILATIONS = (1, 3, 9)
LANES = 128
EDGE = 48
MARGIN = (40, 32, 0)
WIDER = (48, 32, 0)
CORE = 160
FIRST_TAPS = ((0, 4), (4, 7))
SQUARE = (9.869524955749512, -32.46514129638672, 42.64342498779297, -29.426273345947266, 10.581298828125)


def snake(values, frequency, inverse):
    turns = values * frequency
    rest = turns - jnp.round(turns)
    square = rest * rest
    poly = SQUARE[-1]
    for coefficient in SQUARE[-2::-1]:
        poly = poly * square + coefficient
    return values + (poly * square) * inverse


def kernel(
    count, frames,
    up_hbm, taps_hbm, bias_wide_hbm, point_hbm, bias_point_hbm,
    alpha_in_hbm, beta_in_hbm, alpha_mid_hbm, beta_mid_hbm,
    out_ref,
    taps_ref, point_ref, ext_ref, x_ref, s_refs,
    bias_wide, bias_point, alpha_in, beta_in, alpha_mid, beta_mid,
    taps_sems, point_sems, small_sems, up_sem, send_sems, recv_sems,
):
    channels = ext_ref.shape[2]
    groups = channels // LANES
    below, above = EDGE, EDGE + frames
    extended = frames + 2 * EDGE
    me = lax.axis_index("tm")
    has_left = me > 0
    has_right = me < count - 1
    barrier = pltpu.get_barrier_semaphore()

    @pl.when(has_left)
    def _():
        pl.semaphore_signal(barrier, inc=1, device_id={"tm": me - 1}, device_id_type=MESH)

    @pl.when(has_right)
    def _():
        pl.semaphore_signal(barrier, inc=1, device_id={"tm": me + 1}, device_id_type=MESH)

    own = pltpu.make_async_copy(up_hbm, ext_ref.at[:, pl.ds(below, frames), :], up_sem)
    own.start()
    smalls = [
        pltpu.make_async_copy(source, target, small_sems.at[i])
        for i, (source, target) in enumerate((
            (alpha_in_hbm, alpha_in), (beta_in_hbm, beta_in), (bias_wide_hbm, bias_wide),
            (alpha_mid_hbm, alpha_mid), (beta_mid_hbm, beta_mid), (bias_point_hbm, bias_point),
        ))
    ]
    for copy in smalls:
        copy.start()

    def tap_copy(unit, k):
        span = pl.ds(k * channels, channels)
        return pltpu.make_async_copy(
            taps_hbm.at[unit, span, :], taps_ref.at[unit, span, :], taps_sems.at[unit, k]
        )

    tap_copies = [[tap_copy(unit, k) for k in range(KERNEL)] for unit in range(UNITS)]
    point_copies = [
        pltpu.make_async_copy(point_hbm.at[unit], point_ref.at[unit], point_sems.at[unit])
        for unit in range(UNITS)
    ]
    for copy in tap_copies[0]:
        copy.start()
    point_copies[0].start()

    @pl.when(has_left & has_right)
    def _():
        pl.semaphore_wait(barrier, 2)

    @pl.when(has_left != has_right)
    def _():
        pl.semaphore_wait(barrier, 1)

    to_right = pltpu.make_async_remote_copy(
        src_ref=up_hbm.at[:, pl.ds(frames - EDGE, EDGE), :],
        dst_ref=ext_ref.at[:, pl.ds(0, EDGE), :],
        send_sem=send_sems.at[0], recv_sem=recv_sems.at[0],
        device_id={"tm": me + 1}, device_id_type=MESH,
    )
    to_left = pltpu.make_async_remote_copy(
        src_ref=up_hbm.at[:, pl.ds(0, EDGE), :],
        dst_ref=ext_ref.at[:, pl.ds(above, EDGE), :],
        send_sem=send_sems.at[1], recv_sem=recv_sems.at[1],
        device_id={"tm": me - 1}, device_id_type=MESH,
    )

    @pl.when(has_right)
    def _():
        to_right.start()

    @pl.when(has_left)
    def _():
        to_left.start()

    for unit in range(1, UNITS):
        for copy in tap_copies[unit]:
            copy.start()
        point_copies[unit].start()

    @pl.when(jnp.logical_not(has_left))
    def _():
        ext_ref[:, 0:EDGE, :] = jnp.zeros((2, EDGE, channels), jnp.bfloat16)

    @pl.when(jnp.logical_not(has_right))
    def _():
        ext_ref[:, above:extended, :] = jnp.zeros((2, EDGE, channels), jnp.bfloat16)

    def row_of(ref, unit):
        return ref[unit : unit + 1, :]

    def blocks(low, high):
        edges = [low, *range(low - low % 16 + 16, high, 16), high]
        return zip(edges[:-1], edges[1:])

    def hold(unit, low, high, values):
        s = snake(values, row_of(alpha_in, unit) * (1.0 / math.pi), 1.0 / row_of(beta_in, unit))
        if high <= below:
            s = jnp.where(has_left, s, 0.0)
        elif low >= above:
            s = jnp.where(has_right, s, 0.0)
        for c in range(groups):
            part = slice(c * LANES, (c + 1) * LANES)
            x_ref[c, low:high, :] = values[:, part]
            s_refs[unit, c, low:high, :] = s[:, part]

    def enter(low, high):
        for start, stop in blocks(low, high):
            whole = start - start % 16
            early = ext_ref[0, whole : whole + 16, :].astype(jnp.float32)
            if whole:
                late = ext_ref[1, whole - 16 : whole + 16, :].astype(jnp.float32)[8:24]
            else:
                late = ext_ref[1, 0:16, :].astype(jnp.float32)
                late = jnp.concatenate([late[0:8], late[0:8]], axis=0)
            x = (early + late)[start - whole : stop - whole]
            hold(0, start, stop, x.astype(jnp.bfloat16).astype(jnp.float32))

    def shifted(unit, pieces, first, last):
        columns = []
        for k in range(first, last):
            offset = (k - KERNEL // 2) * DILATIONS[unit]
            rows = [
                jnp.concatenate(
                    [s_refs[unit, c, low + offset : high + offset, :] for c in range(groups)], axis=1
                )
                for low, high in pieces
            ]
            columns.append(jnp.concatenate(rows, axis=0).astype(jnp.bfloat16))
        return jnp.concatenate(columns, axis=1)

    def wide(unit, pieces, first=0, last=KERNEL):
        weights = taps_ref[unit, first * channels : last * channels, :]
        return jnp.dot(shifted(unit, pieces, first, last), weights, preferred_element_type=jnp.float32)

    def close(unit, pieces, h):
        h = h + row_of(bias_wide, unit)
        g = snake(h, row_of(alpha_mid, unit) * (1.0 / math.pi), 1.0 / row_of(beta_mid, unit))
        update = jnp.dot(g.astype(jnp.bfloat16), point_ref[unit], preferred_element_type=jnp.float32)
        update = update + row_of(bias_point, unit)
        base = 0
        for low, high in pieces:
            for start, stop in blocks(low, high):
                kept = jnp.concatenate([x_ref[c, start:stop, :] for c in range(groups)], axis=1)
                at = base + start - low
                x = (kept + update[at : at + stop - start]).astype(jnp.bfloat16)
                if unit + 1 < UNITS:
                    hold(unit + 1, start, stop, x.astype(jnp.float32))
                else:
                    out_ref[start - below : stop - below, :] = x
            base += high - low

    middle = extended // 2
    cores, rims = [], []
    for unit in range(UNITS):
        low, high = middle - CORE // 2 - WIDER[unit], middle + CORE // 2 + WIDER[unit]
        cores.append(((low, high),))
        rims.append(((below - MARGIN[unit], low), (high, above + MARGIN[unit])))
    inside = (cores[0][0][0] - 16, cores[0][0][1] + 16)

    for copy in smalls:
        copy.wait()
    own.wait()
    enter(*inside)
    core = None
    for first, last in FIRST_TAPS:
        for copy in tap_copies[0][first:last]:
            copy.wait()
        if last == KERNEL:
            point_copies[0].wait()

            @pl.when(has_left)
            def _():
                to_right.wait_recv()

            @pl.when(has_right)
            def _():
                to_left.wait_recv()

        part = wide(0, cores[0], first, last)
        core = part if core is None else core + part
    enter(below - MARGIN[0], inside[0])
    enter(inside[1], above + MARGIN[0])
    rim = None
    for unit in range(UNITS):
        if unit:
            for copy in tap_copies[unit]:
                copy.wait()
            point_copies[unit].wait()
            core = wide(unit, cores[unit])
            close(unit - 1, rims[unit - 1], rim)
        rim = wide(unit, rims[unit])
        close(unit, cores[unit], core)
    close(UNITS - 1, rims[UNITS - 1], rim)

    @pl.when(has_right)
    def _():
        to_right.wait_send()

    @pl.when(has_left)
    def _():
        to_left.wait_send()


def land(held_ref, out_hbm, sem):
    copy = pltpu.make_async_copy(held_ref, out_hbm, sem)
    copy.start()
    copy.wait()


def per_device(
    upsampled, taps, bias_wide, pointwise, bias_point, alpha_in, beta_in, alpha_mid, beta_mid
):
    count = lax.axis_size("tm")
    frames, channels = upsampled.shape[1:]
    extended = frames + 2 * EDGE
    hbm = pl.BlockSpec(memory_space=pltpu.HBM)
    return pl.pallas_call(
        functools.partial(kernel, count, frames),
        out_shape=pltpu.VMEM((frames, channels), jnp.bfloat16),
        in_specs=[hbm] * 9,
        out_specs=pl.BlockSpec(memory_space=pltpu.VMEM),
        scratch_shapes=[
            pltpu.VMEM((UNITS, KERNEL * channels, channels), jnp.bfloat16),
            pltpu.VMEM((UNITS, channels, channels), jnp.bfloat16),
            pltpu.VMEM((2, extended, channels), jnp.bfloat16),
            pltpu.VMEM((channels // LANES, extended, LANES), jnp.float32),
            pltpu.VMEM((UNITS, channels // LANES, extended, LANES), jnp.float32),
        ]
        + [pltpu.VMEM((UNITS, channels), jnp.float32)] * 6
        + [
            pltpu.SemaphoreType.DMA((UNITS, KERNEL)),
            pltpu.SemaphoreType.DMA((UNITS,)),
            pltpu.SemaphoreType.DMA((6,)),
            pltpu.SemaphoreType.DMA,
            pltpu.SemaphoreType.DMA((2,)),
            pltpu.SemaphoreType.DMA((2,)),
        ],
        compiler_params=pltpu.CompilerParams(
            vmem_limit_bytes=58000000, collective_id=0, has_side_effects=True
        ),
    )(
        upsampled, taps.reshape(UNITS, KERNEL * channels, channels), bias_wide, pointwise,
        bias_point, alpha_in, beta_in, alpha_mid, beta_mid,
    )


def solution(mesh):
    placed = (P(None, ("grp", "tm"), None), P(), P(), P(), P(), P(), P(), P(), P())
    return jax.shard_map(
        per_device, mesh=mesh, in_specs=placed, out_specs=P(("grp", "tm"), None), check_vma=False
    )
```

```python
import functools
import math

import jax
import jax.numpy as jnp
from jax import lax
from jax.experimental import pallas as pl
from jax.experimental.pallas import tpu as pltpu
from jax.sharding import PartitionSpec as P

MESH = pl.DeviceIdType.MESH
KERNEL = 7
STRIDE = 8
UNITS = 3
DILATIONS = (1, 3, 9)
LANES = 128
TILE = 16
EDGE = 48
MARGIN = (40, 32, 0)
INSET = (64, 80, 112)
LEFT = (13, 11, 7)
STEP = 256
SQUARE = (9.869524955749512, -32.46514129638672, 42.64342498779297, -29.426273345947266, 10.581298828125)


def snake(values, frequency, inverse):
    turns = values * frequency
    rest = turns - jnp.round(turns)
    square = rest * rest
    poly = SQUARE[-1]
    for coefficient in SQUARE[-2::-1]:
        poly = poly * square + coefficient
    return values + (poly * square) * inverse


def blocks(low, high):
    edges = [low, *range(low - low % TILE + TILE, high, TILE), high]
    return list(zip(edges[:-1], edges[1:]))


def kernel(
    count, frames, gated_at,
    up_hbm, taps_hbm, bias_wide_hbm, point_hbm, bias_point_hbm,
    alpha_in_hbm, beta_in_hbm, alpha_mid_hbm, beta_mid_hbm,
    out_ref,
    taps_ref, point_ref, up_ref, leave_ref, halo_ref, x_ref, held_ref,
    bias_wide, bias_point, alpha_in, beta_in, alpha_mid, beta_mid,
    taps_sems, point_sems, small_sems, up_sem, send_sems, recv_sems,
):
    channels = up_ref.shape[2]
    groups = channels // LANES
    below, above = EDGE, EDGE + frames
    extended = frames + 2 * EDGE
    me = lax.axis_index("tm")
    has_left = me > 0
    has_right = me < count - 1
    none = pl.multiple_of((me // 1024) * 8, 8)
    barrier = pltpu.get_barrier_semaphore()

    @pl.when(has_left)
    def _():
        pl.semaphore_signal(barrier, inc=1, device_id={"tm": me - 1}, device_id_type=MESH)

    @pl.when(has_right)
    def _():
        pl.semaphore_signal(barrier, inc=1, device_id={"tm": me + 1}, device_id_type=MESH)

    own = pltpu.make_async_copy(up_hbm, up_ref, up_sem)
    own.start()
    smalls = [
        pltpu.make_async_copy(source, target, small_sems.at[i])
        for i, (source, target) in enumerate((
            (alpha_in_hbm, alpha_in), (beta_in_hbm, beta_in), (bias_wide_hbm, bias_wide),
            (alpha_mid_hbm, alpha_mid), (beta_mid_hbm, beta_mid), (bias_point_hbm, bias_point),
        ))
    ]
    for copy in smalls:
        copy.start()

    def tap_copy(unit, k):
        span = pl.ds(k * channels, channels)
        return pltpu.make_async_copy(
            taps_hbm.at[unit, span, :], taps_ref.at[unit, span, :], taps_sems.at[unit, k]
        )

    weights = []
    for unit in range(UNITS):
        point = pltpu.make_async_copy(point_hbm.at[unit], point_ref.at[unit], point_sems.at[unit])
        weights.append([*(tap_copy(unit, k) for k in range(KERNEL)), point])
    for copy in weights[0]:
        copy.start()

    to_right = pltpu.make_async_remote_copy(
        src_ref=leave_ref.at[0], dst_ref=halo_ref.at[0],
        send_sem=send_sems.at[0], recv_sem=recv_sems.at[0],
        device_id={"tm": me + 1}, device_id_type=MESH,
    )
    to_left = pltpu.make_async_remote_copy(
        src_ref=leave_ref.at[1], dst_ref=halo_ref.at[1],
        send_sem=send_sems.at[1], recv_sem=recv_sems.at[1],
        device_id={"tm": me - 1}, device_id_type=MESH,
    )

    @pl.when(jnp.logical_not(has_left))
    def _():
        halo_ref[0] = jnp.zeros(halo_ref.shape[1:], jnp.bfloat16)

    @pl.when(jnp.logical_not(has_right))
    def _():
        halo_ref[1] = jnp.zeros(halo_ref.shape[1:], jnp.bfloat16)

    def wide_rows(ref, part, low, high):
        start, stop = low - low % TILE, high + (-high) % TILE
        return ref[part, start:stop, :].astype(jnp.float32)[low - start : high - start]

    def rounded(values):
        return values.astype(jnp.bfloat16).astype(jnp.float32)

    def summed(low, high):
        return rounded(wide_rows(up_ref, 0, low, high) + wide_rows(up_ref, 1, low - STRIDE, high - STRIDE))

    def row_of(ref, unit):
        return ref[unit : unit + 1, :]

    def hold(unit, low, high, values):
        s = snake(values, row_of(alpha_in, unit) * (1.0 / math.pi), 1.0 / row_of(beta_in, unit))
        if high <= below:
            s = jnp.where(has_left, s, 0.0)
        elif low >= above:
            s = jnp.where(has_right, s, 0.0)
        for c in range(groups):
            part = slice(c * LANES, (c + 1) * LANES)
            x_ref[c, low:high, :] = values[:, part]
            held_ref[c, pl.ds(none + (unit * extended + low), high - low), :] = s[:, part]

    def enter(low, high):
        def one(start, stop):
            hold(0, start, stop, summed(start - below, stop - below))
        return [functools.partial(one, *span) for span in blocks(low, high)]

    def enter_halo():
        def first():
            early = wide_rows(up_ref, 0, 0, STRIDE)
            hold(0, below, below + STRIDE, rounded(early + wide_rows(halo_ref, 0, 0, STRIDE)))
        def last():
            late = wide_rows(up_ref, 1, frames - STRIDE, frames)
            hold(0, above, above + STRIDE, rounded(wide_rows(halo_ref, 1, 0, STRIDE) + late))
        def lower(start, stop):
            hold(0, start, stop, wide_rows(halo_ref, 0, start, stop))
        def upper(start, stop):
            hold(0, start, stop, wide_rows(halo_ref, 1, start - above, stop - above))
        return [
            first, last,
            *(functools.partial(lower, *span) for span in blocks(below - MARGIN[0], below)),
            *(functools.partial(upper, *span) for span in blocks(above + STRIDE, above + MARGIN[0])),
        ]

    def rows_of(first, pieces, channel):
        found = [
            jnp.concatenate(
                [held_ref[c, first + low : first + high, :] for c in range(channel // LANES, (channel + STEP) // LANES)],
                axis=1,
            )
            for low, high in pieces
        ]
        return jnp.concatenate(found, axis=0).astype(jnp.bfloat16)

    def conv_steps(unit, pieces):
        def one(k, channel, total):
            first = unit * extended + (k - KERNEL // 2) * DILATIONS[unit]
            at = k * channels + channel
            part = jnp.dot(
                rows_of(first, pieces, channel), taps_ref[unit, at : at + STEP, :],
                preferred_element_type=jnp.float32,
            )
            return part if total is None else total + part
        return [
            functools.partial(one, k, channel)
            for k in range(KERNEL) for channel in range(0, channels, STEP)
        ]

    def mid_tasks(unit, pieces, h):
        def one(start, stop):
            g = snake(
                h[start:stop] + row_of(bias_wide, unit),
                row_of(alpha_mid, unit) * (1.0 / math.pi), 1.0 / row_of(beta_mid, unit),
            )
            for c in range(groups):
                held_ref[c, pl.ds(none + (gated_at + start), stop - start), :] = g[:, c * LANES : (c + 1) * LANES]
        return [functools.partial(one, *span) for span in blocks(0, h.shape[0])]

    def point(unit, size):
        total = None
        for channel in range(0, channels, STEP):
            part = jnp.dot(
                rows_of(gated_at, ((0, size),), channel), point_ref[unit, channel : channel + STEP, :],
                preferred_element_type=jnp.float32,
            )
            total = part if total is None else total + part
        return total

    def end_tasks(unit, pieces, update):
        def one(at, start, stop):
            kept = jnp.concatenate([x_ref[c, start:stop, :] for c in range(groups)], axis=1)
            x = (kept + (update[at : at + stop - start] + row_of(bias_point, unit))).astype(jnp.bfloat16)
            if unit + 1 < UNITS:
                hold(unit + 1, start, stop, x.astype(jnp.float32))
            else:
                out_ref[start - below : stop - below, :] = x
        tasks, base = [], 0
        for low, high in pieces:
            tasks += [functools.partial(one, base + start - low, start, stop) for start, stop in blocks(low, high)]
            base += high - low
        return tasks

    def size_of(pieces):
        return sum(high - low for low, high in pieces)

    left, right, rims = [], [], []
    for unit in range(UNITS):
        low, high = INSET[unit], extended - INSET[unit]
        cut = low + LEFT[unit] * TILE
        left.append((unit, ((low, cut),)))
        right.append((unit, ((cut, high),)))
        rims.append((unit, ((below - MARGIN[unit], low), (high, above + MARGIN[unit]))))

    def run(steps, tasks, total=None):
        done = 0
        for i, step in enumerate(steps):
            total = step(total)
            upto = (i + 1) * len(tasks) // len(steps)
            for task in tasks[done:upto]:
                task()
            done = upto
        return total

    def stage(this, before, h, also=(), waits=()):
        unit, pieces = this
        steps = conv_steps(unit, pieces)
        half = len(steps) // 2
        if before is None:
            total = None
            each = len(steps) // KERNEL
            for k in range(KERNEL):
                waits[k].wait()
                total = run(steps[k * each : (k + 1) * each], also[k * len(also) // KERNEL : (k + 1) * len(also) // KERNEL], total)
            return total
        total = run(steps[:half], mid_tasks(*before, h))
        update = point(before[0], size_of(before[1]))
        return run(steps[half:], [*end_tasks(*before, update), *also], total)

    own.wait()
    for copy in smalls:
        copy.wait()
    tail = frames - EDGE
    for side, start in ((0, tail), (1, 0)):
        for block in range(0, EDGE, TILE):
            if block:
                rows = summed(start + block, start + block + TILE)
            else:
                if side == 0:
                    raw = wide_rows(up_ref, 1, frames - STRIDE, frames)
                else:
                    raw = wide_rows(up_ref, 0, 0, STRIDE)
                rows = jnp.concatenate([raw, summed(start + STRIDE, start + TILE)], axis=0)
            leave_ref[side, block : block + TILE, :] = rows.astype(jnp.bfloat16)

    cut = left[0][1][0][1]
    for task in enter(below + STRIDE, cut + TILE):
        task()
    for copy in weights[1]:
        copy.start()
    h = stage(left[0], None, None, enter(cut + TILE, above), weights[0])
    weights[0][KERNEL].wait()

    @pl.when(has_left & has_right)
    def _():
        pl.semaphore_wait(barrier, 2)

    @pl.when(has_left != has_right)
    def _():
        pl.semaphore_wait(barrier, 1)

    @pl.when(has_right)
    def _():
        to_right.start()

    @pl.when(has_left)
    def _():
        to_left.start()

    for copy in weights[2]:
        copy.start()
    h = stage(right[0], left[0], h)
    for copy in weights[1]:
        copy.wait()
    h = stage(left[1], right[0], h)
    h = stage(right[1], left[1], h)

    @pl.when(has_left)
    def _():
        to_right.wait_recv()

    @pl.when(has_right)
    def _():
        to_left.wait_recv()

    for task in enter_halo():
        task()
    h = stage(rims[0], right[1], h)
    for copy in weights[2]:
        copy.wait()
    h = stage(left[2], rims[0], h)
    h = stage(rims[1], left[2], h)
    h = stage(right[2], rims[1], h)
    h = stage(rims[2], right[2], h)
    for task in mid_tasks(*rims[2], h):
        task()
    for task in end_tasks(*rims[2], point(UNITS - 1, size_of(rims[2][1]))):
        task()

    @pl.when(has_right)
    def _():
        to_right.wait_send()

    @pl.when(has_left)
    def _():
        to_left.wait_send()


def per_device(
    upsampled, taps, bias_wide, pointwise, bias_point, alpha_in, beta_in, alpha_mid, beta_mid
):
    count = lax.axis_size("tm")
    frames, channels = upsampled.shape[1:]
    extended = frames + 2 * EDGE
    gated_at = UNITS * extended
    hbm = pl.BlockSpec(memory_space=pltpu.HBM)
    return pl.pallas_call(
        functools.partial(kernel, count, frames, gated_at),
        out_shape=pltpu.VMEM((frames, channels), jnp.bfloat16),
        in_specs=[hbm] * 9,
        out_specs=pl.BlockSpec(memory_space=pltpu.VMEM),
        scratch_shapes=[
            pltpu.VMEM((UNITS, KERNEL * channels, channels), jnp.bfloat16),
            pltpu.VMEM((UNITS, channels, channels), jnp.bfloat16),
            pltpu.VMEM((2, frames, channels), jnp.bfloat16),
            pltpu.VMEM((2, EDGE, channels), jnp.bfloat16),
            pltpu.VMEM((2, EDGE, channels), jnp.bfloat16),
            pltpu.VMEM((channels // LANES, extended, LANES), jnp.float32),
            pltpu.VMEM((channels // LANES, gated_at + extended, LANES), jnp.float32),
        ]
        + [pltpu.VMEM((UNITS, channels), jnp.float32)] * 6
        + [
            pltpu.SemaphoreType.DMA((UNITS, KERNEL)),
            pltpu.SemaphoreType.DMA((UNITS,)),
            pltpu.SemaphoreType.DMA((6,)),
            pltpu.SemaphoreType.DMA,
            pltpu.SemaphoreType.DMA((2,)),
            pltpu.SemaphoreType.DMA((2,)),
        ],
        compiler_params=pltpu.CompilerParams(
            vmem_limit_bytes=58_000_000, collective_id=0, has_side_effects=True
        ),
    )(
        upsampled, taps.reshape(UNITS, KERNEL * channels, channels), bias_wide, pointwise,
        bias_point, alpha_in, beta_in, alpha_mid, beta_mid,
    )


def solution(mesh):
    placed = (P(None, ("grp", "tm"), None), P(), P(), P(), P(), P(), P(), P(), P())
    return jax.shard_map(
        per_device, mesh=mesh, in_specs=placed, out_specs=P(("grp", "tm"), None), check_vma=False
    )
```

```python
import functools
import math

import jax
import jax.numpy as jnp
from jax import lax
from jax.experimental import pallas as pl
from jax.experimental.pallas import tpu as pltpu
from jax.sharding import PartitionSpec as P

MESH = pl.DeviceIdType.MESH
KERNEL = 7
STRIDE = 8
UNITS = 3
DILATIONS = (1, 3, 9)
LANES = 128
TILE = 16
EDGE = 48
MARGIN = (40, 32, 0)
INSET = (64, 80, 112)
LEFT = (13, 11, 7)
STEP = 256
SQUARE = (9.869524955749512, -32.46514129638672, 42.64342498779297, -29.426273345947266, 10.581298828125)


def snake(values, frequency, inverse):
    turns = values * frequency
    rest = turns - jnp.round(turns)
    square = rest * rest
    poly = SQUARE[-1]
    for coefficient in SQUARE[-2::-1]:
        poly = poly * square + coefficient
    return values + poly * (square * inverse)


def blocks(low, high):
    edges = [low, *range(low - low % TILE + TILE, high, TILE), high]
    return list(zip(edges[:-1], edges[1:]))


def kernel(
    count, frames, gated_at,
    up_hbm, taps_hbm, bias_wide_hbm, point_hbm, bias_point_hbm,
    alpha_in_hbm, beta_in_hbm, alpha_mid_hbm, beta_mid_hbm,
    out_ref,
    taps_ref, point_ref, up_ref, halo_ref, x_ref, held_ref,
    bias_wide, bias_point, alpha_in, beta_in, alpha_mid, beta_mid,
    taps_sems, point_sems, small_sems, up_sem, send_sems, recv_sems,
):
    channels = up_ref.shape[2]
    groups = channels // LANES
    below, above = EDGE, EDGE + frames
    extended = frames + 2 * EDGE
    me = lax.axis_index("tm")
    has_left = me > 0
    has_right = me < count - 1
    none = pl.multiple_of((me // 1024) * 8, 8)
    barrier = pltpu.get_barrier_semaphore()

    @pl.when(has_left)
    def _():
        pl.semaphore_signal(barrier, inc=1, device_id={"tm": me - 1}, device_id_type=MESH)

    @pl.when(has_right)
    def _():
        pl.semaphore_signal(barrier, inc=1, device_id={"tm": me + 1}, device_id_type=MESH)

    own = pltpu.make_async_copy(up_hbm, up_ref, up_sem)
    own.start()
    smalls = [
        pltpu.make_async_copy(source, target, small_sems.at[i])
        for i, (source, target) in enumerate((
            (alpha_in_hbm, alpha_in), (beta_in_hbm, beta_in), (bias_wide_hbm, bias_wide),
            (alpha_mid_hbm, alpha_mid), (beta_mid_hbm, beta_mid), (bias_point_hbm, bias_point),
        ))
    ]
    for copy in smalls:
        copy.start()

    def tap_copy(unit, k):
        span = pl.ds(k * channels, channels)
        return pltpu.make_async_copy(
            taps_hbm.at[unit, span, :], taps_ref.at[unit, span, :], taps_sems.at[unit, k]
        )

    weights = []
    for unit in range(UNITS):
        point = pltpu.make_async_copy(point_hbm.at[unit], point_ref.at[unit], point_sems.at[unit])
        weights.append([*(tap_copy(unit, k) for k in range(KERNEL)), point])
    for copy in weights[0]:
        copy.start()

    to_right = pltpu.make_async_remote_copy(
        src_ref=up_hbm.at[:, pl.ds(frames - EDGE, EDGE), :], dst_ref=halo_ref.at[0],
        send_sem=send_sems.at[0], recv_sem=recv_sems.at[0],
        device_id={"tm": me + 1}, device_id_type=MESH,
    )
    to_left = pltpu.make_async_remote_copy(
        src_ref=up_hbm.at[:, pl.ds(0, EDGE), :], dst_ref=halo_ref.at[1],
        send_sem=send_sems.at[1], recv_sem=recv_sems.at[1],
        device_id={"tm": me - 1}, device_id_type=MESH,
    )

    @pl.when(jnp.logical_not(has_left))
    def _():
        halo_ref[0] = jnp.zeros(halo_ref.shape[1:], jnp.bfloat16)

    @pl.when(jnp.logical_not(has_right))
    def _():
        halo_ref[1] = jnp.zeros(halo_ref.shape[1:], jnp.bfloat16)

    def wide_rows(ref, part, low, high):
        start, stop = low - low % TILE, high + (-high) % TILE
        return ref[part, start:stop, :].astype(jnp.float32)[low - start : high - start]

    def rounded(values):
        return values.astype(jnp.bfloat16).astype(jnp.float32)

    def summed(low, high):
        return rounded(wide_rows(up_ref, 0, low, high) + wide_rows(up_ref, 1, low - STRIDE, high - STRIDE))

    def row_of(ref, unit):
        return ref[unit : unit + 1, :]

    def hold(unit, low, high, values):
        s = snake(values, row_of(alpha_in, unit) * (1.0 / math.pi), 1.0 / row_of(beta_in, unit))
        if high <= below:
            s = jnp.where(has_left, s, 0.0)
        elif low >= above:
            s = jnp.where(has_right, s, 0.0)
        for c in range(groups):
            part = slice(c * LANES, (c + 1) * LANES)
            x_ref[c, low:high, :] = values[:, part]
            held_ref[c, pl.ds(none + (unit * extended + low), high - low), :] = s[:, part]

    def enter(low, high):
        def one(start, stop):
            hold(0, start, stop, summed(start - below, stop - below))
        return [functools.partial(one, *span) for span in blocks(low, high)]

    def enter_halo():
        near, far = [
            [halo_ref[side, part].astype(jnp.float32) for part in range(2)] for side in range(2)
        ]
        early = wide_rows(up_ref, 0, 0, STRIDE)
        late = wide_rows(up_ref, 1, frames - STRIDE, frames)
        late_near = jnp.concatenate([near[1][0:STRIDE], near[1]], axis=0)[0:EDGE]
        lower = near[0] + late_near
        upper = far[0] + jnp.concatenate([late, far[1]], axis=0)[0:EDGE]
        for start, stop in blocks(below - MARGIN[0], below):
            hold(0, start, stop, rounded(lower[start:stop]))
        hold(0, below, below + STRIDE, rounded(early + near[1][EDGE - STRIDE : EDGE]))
        for start, stop in blocks(above, above + MARGIN[0]):
            hold(0, start, stop, rounded(upper[start - above : stop - above]))

    def rows_of(first, pieces, channel):
        found = [
            jnp.concatenate(
                [held_ref[c, first + low : first + high, :] for c in range(channel // LANES, (channel + STEP) // LANES)],
                axis=1,
            )
            for low, high in pieces
        ]
        return jnp.concatenate(found, axis=0).astype(jnp.bfloat16)

    def conv_steps(unit, pieces):
        def one(k, channel, total):
            first = unit * extended + (k - KERNEL // 2) * DILATIONS[unit]
            at = k * channels + channel
            part = jnp.dot(
                rows_of(first, pieces, channel), taps_ref[unit, at : at + STEP, :],
                preferred_element_type=jnp.float32,
            )
            return part if total is None else total + part
        return [
            functools.partial(one, k, channel)
            for k in range(KERNEL) for channel in range(0, channels, STEP)
        ]

    def mid_tasks(unit, pieces, h):
        def one(start, stop):
            g = snake(
                h[start:stop] + row_of(bias_wide, unit),
                row_of(alpha_mid, unit) * (1.0 / math.pi), 1.0 / row_of(beta_mid, unit),
            )
            for c in range(groups):
                held_ref[c, pl.ds(none + (gated_at + start), stop - start), :] = g[:, c * LANES : (c + 1) * LANES]
        return [functools.partial(one, *span) for span in blocks(0, h.shape[0])]

    def point(unit, size):
        total = None
        for channel in range(0, channels, STEP):
            part = jnp.dot(
                rows_of(gated_at, ((0, size),), channel), point_ref[unit, channel : channel + STEP, :],
                preferred_element_type=jnp.float32,
            )
            total = part if total is None else total + part
        return total

    def end_tasks(unit, pieces, update):
        def one(at, start, stop):
            kept = jnp.concatenate([x_ref[c, start:stop, :] for c in range(groups)], axis=1)
            x = (kept + (update[at : at + stop - start] + row_of(bias_point, unit))).astype(jnp.bfloat16)
            if unit + 1 < UNITS:
                hold(unit + 1, start, stop, x.astype(jnp.float32))
            else:
                out_ref[start - below : stop - below, :] = x
        tasks, base = [], 0
        for low, high in pieces:
            tasks += [functools.partial(one, base + start - low, start, stop) for start, stop in blocks(low, high)]
            base += high - low
        return tasks

    def size_of(pieces):
        return sum(high - low for low, high in pieces)

    core = ((below + STRIDE + TILE // 2, above - TILE),)
    rims = ((below - MARGIN[0], core[0][0]), (core[0][1], above + MARGIN[0]))
    wholes = [((below - MARGIN[unit], above + MARGIN[unit]),) for unit in range(UNITS)]

    def conv(unit, pieces, waits=None):
        total = None
        steps = conv_steps(unit, pieces)
        each = len(steps) // KERNEL
        for k in range(KERNEL):
            if waits is not None:
                waits[k].wait()
            for step in steps[k * each : (k + 1) * each]:
                total = step(total)
        return total

    def close(unit, pieces, h):
        for task in mid_tasks(unit, pieces, h):
            task()
        for task in end_tasks(unit, pieces, point(unit, size_of(pieces))):
            task()

    @pl.when(has_left & has_right)
    def _():
        pl.semaphore_wait(barrier, 2)

    @pl.when(has_left != has_right)
    def _():
        pl.semaphore_wait(barrier, 1)

    @pl.when(has_right)
    def _():
        to_right.start()

    @pl.when(has_left)
    def _():
        to_left.start()

    own.wait()
    for copy in smalls:
        copy.wait()
    for task in enter(below + STRIDE, above):
        task()
    for copy in weights[1]:
        copy.start()
    h = conv(0, core, weights[0])
    weights[0][KERNEL].wait()
    for copy in weights[2]:
        copy.start()
    close(0, core, h)

    @pl.when(has_left)
    def _():
        to_right.wait_recv()

    @pl.when(has_right)
    def _():
        to_left.wait_recv()

    enter_halo()
    close(0, rims, conv(0, rims))
    for unit in range(1, UNITS):
        for copy in weights[unit]:
            copy.wait()
        close(unit, wholes[unit], conv(unit, wholes[unit]))

    @pl.when(has_right)
    def _():
        to_right.wait_send()

    @pl.when(has_left)
    def _():
        to_left.wait_send()


def per_device(
    upsampled, taps, bias_wide, pointwise, bias_point, alpha_in, beta_in, alpha_mid, beta_mid
):
    count = lax.axis_size("tm")
    frames, channels = upsampled.shape[1:]
    extended = frames + 2 * EDGE
    gated_at = UNITS * extended
    hbm = pl.BlockSpec(memory_space=pltpu.HBM)
    return pl.pallas_call(
        functools.partial(kernel, count, frames, gated_at),
        out_shape=pltpu.VMEM((frames, channels), jnp.bfloat16),
        in_specs=[hbm] * 9,
        out_specs=pl.BlockSpec(memory_space=pltpu.VMEM),
        scratch_shapes=[
            pltpu.VMEM((UNITS, KERNEL * channels, channels), jnp.bfloat16),
            pltpu.VMEM((UNITS, channels, channels), jnp.bfloat16),
            pltpu.VMEM((2, frames, channels), jnp.bfloat16),
            pltpu.VMEM((2, 2, EDGE, channels), jnp.bfloat16),
            pltpu.VMEM((channels // LANES, extended, LANES), jnp.float32),
            pltpu.VMEM((channels // LANES, gated_at + extended, LANES), jnp.float32),
        ]
        + [pltpu.VMEM((UNITS, channels), jnp.float32)] * 6
        + [
            pltpu.SemaphoreType.DMA((UNITS, KERNEL)),
            pltpu.SemaphoreType.DMA((UNITS,)),
            pltpu.SemaphoreType.DMA((6,)),
            pltpu.SemaphoreType.DMA,
            pltpu.SemaphoreType.DMA((2,)),
            pltpu.SemaphoreType.DMA((2,)),
        ],
        compiler_params=pltpu.CompilerParams(
            vmem_limit_bytes=58_000_000, collective_id=0, has_side_effects=True
        ),
    )(
        upsampled, taps.reshape(UNITS, KERNEL * channels, channels), bias_wide, pointwise,
        bias_point, alpha_in, beta_in, alpha_mid, beta_mid,
    )


def solution(mesh):
    placed = (P(None, ("grp", "tm"), None), P(), P(), P(), P(), P(), P(), P(), P())
    return jax.shard_map(
        per_device, mesh=mesh, in_specs=placed, out_specs=P(("grp", "tm"), None), check_vma=False
    )
```

```python
import functools
import math

import jax
import jax.numpy as jnp
from jax import lax
from jax.experimental import pallas as pl
from jax.experimental.pallas import tpu as pltpu
from jax.sharding import PartitionSpec as P

MESH = pl.DeviceIdType.MESH
KERNEL = 7
STRIDE = 8
UNITS = 3
DILATIONS = (1, 3, 9)
LANES = 128
TILE = 16
EDGE = 48
MARGIN = (40, 32, 0)
INSET = (64, 80, 112)
LEFT = (13, 11, 7)
STEP = 256
SQUARE = (9.869524955749512, -32.46514129638672, 42.64342498779297, -29.426273345947266, 10.581298828125)


def snake(values, frequency, inverse):
    turns = values * frequency
    rest = turns - jnp.round(turns)
    square = rest * rest
    poly = SQUARE[-1]
    for coefficient in SQUARE[-2::-1]:
        poly = poly * square + coefficient
    return values + poly * (square * inverse)


def blocks(low, high):
    edges = [low, *range(low - low % TILE + TILE, high, TILE), high]
    return list(zip(edges[:-1], edges[1:]))


def kernel(
    count, frames, gated_at,
    up_hbm, taps_hbm, bias_wide_hbm, point_hbm, bias_point_hbm,
    alpha_in_hbm, beta_in_hbm, alpha_mid_hbm, beta_mid_hbm,
    out_ref,
    taps_ref, point_ref, up_ref, halo_ref, x_ref, held_ref,
    bias_wide, bias_point, alpha_in, beta_in, alpha_mid, beta_mid,
    taps_sems, point_sems, small_sems, up_sem, send_sems, recv_sems,
):
    channels = up_ref.shape[2]
    groups = channels // LANES
    below, above = EDGE, EDGE + frames
    extended = frames + 2 * EDGE
    me = lax.axis_index("tm")
    has_left = me > 0
    has_right = me < count - 1
    none = 0
    barrier = pltpu.get_barrier_semaphore()

    @pl.when(has_left)
    def _():
        pl.semaphore_signal(barrier, inc=1, device_id={"tm": me - 1}, device_id_type=MESH)

    @pl.when(has_right)
    def _():
        pl.semaphore_signal(barrier, inc=1, device_id={"tm": me + 1}, device_id_type=MESH)

    own = pltpu.make_async_copy(up_hbm, up_ref, up_sem)
    own.start()
    smalls = [
        pltpu.make_async_copy(source, target, small_sems.at[i])
        for i, (source, target) in enumerate((
            (alpha_in_hbm, alpha_in), (beta_in_hbm, beta_in), (bias_wide_hbm, bias_wide),
            (alpha_mid_hbm, alpha_mid), (beta_mid_hbm, beta_mid), (bias_point_hbm, bias_point),
        ))
    ]
    for copy in smalls:
        copy.start()

    def tap_copy(unit, k):
        span = pl.ds(k * channels, channels)
        return pltpu.make_async_copy(
            taps_hbm.at[unit, span, :], taps_ref.at[unit, span, :], taps_sems.at[unit, k]
        )

    weights = []
    for unit in range(UNITS):
        point = pltpu.make_async_copy(point_hbm.at[unit], point_ref.at[unit], point_sems.at[unit])
        weights.append([*(tap_copy(unit, k) for k in range(KERNEL)), point])
    for copy in weights[0]:
        copy.start()

    to_right = pltpu.make_async_remote_copy(
        src_ref=up_hbm.at[:, pl.ds(frames - EDGE, EDGE), :], dst_ref=halo_ref.at[0],
        send_sem=send_sems.at[0], recv_sem=recv_sems.at[0],
        device_id={"tm": me + 1}, device_id_type=MESH,
    )
    to_left = pltpu.make_async_remote_copy(
        src_ref=up_hbm.at[:, pl.ds(0, EDGE), :], dst_ref=halo_ref.at[1],
        send_sem=send_sems.at[1], recv_sem=recv_sems.at[1],
        device_id={"tm": me - 1}, device_id_type=MESH,
    )

    @pl.when(jnp.logical_not(has_left))
    def _():
        halo_ref[0] = jnp.zeros(halo_ref.shape[1:], jnp.bfloat16)

    @pl.when(jnp.logical_not(has_right))
    def _():
        halo_ref[1] = jnp.zeros(halo_ref.shape[1:], jnp.bfloat16)

    def wide_rows(ref, part, low, high):
        start, stop = low - low % TILE, high + (-high) % TILE
        return ref[part, start:stop, :].astype(jnp.float32)[low - start : high - start]

    def rounded(values):
        return values.astype(jnp.bfloat16).astype(jnp.float32)

    def summed(low, high):
        return rounded(wide_rows(up_ref, 0, low, high) + wide_rows(up_ref, 1, low - STRIDE, high - STRIDE))

    def row_of(ref, unit):
        return ref[unit : unit + 1, :]

    def hold(unit, low, high, values):
        s = snake(values, row_of(alpha_in, unit) * (1.0 / math.pi), 1.0 / row_of(beta_in, unit))
        if high <= below:
            s = jnp.where(has_left, s, 0.0)
        elif low >= above:
            s = jnp.where(has_right, s, 0.0)
        for c in range(groups):
            part = slice(c * LANES, (c + 1) * LANES)
            x_ref[c, low:high, :] = values[:, part]
            held_ref[c, pl.ds(none + (unit * extended + low), high - low), :] = s[:, part]

    def enter(low, high):
        def one(start, stop):
            hold(0, start, stop, summed(start - below, stop - below))
        return [functools.partial(one, *span) for span in blocks(low, high)]

    def enter_halo():
        near, far = [
            [halo_ref[side, part].astype(jnp.float32) for part in range(2)] for side in range(2)
        ]
        early = wide_rows(up_ref, 0, 0, STRIDE)
        late = wide_rows(up_ref, 1, frames - STRIDE, frames)
        late_near = jnp.concatenate([near[1][0:STRIDE], near[1]], axis=0)[0:EDGE]
        lower = near[0] + late_near
        upper = far[0] + jnp.concatenate([late, far[1]], axis=0)[0:EDGE]
        for start, stop in blocks(below - MARGIN[0], below):
            hold(0, start, stop, rounded(lower[start:stop]))
        hold(0, below, below + STRIDE, rounded(early + near[1][EDGE - STRIDE : EDGE]))
        for start, stop in blocks(above, above + MARGIN[0]):
            hold(0, start, stop, rounded(upper[start - above : stop - above]))

    def rows_of(first, pieces, channel):
        found = [
            jnp.concatenate(
                [held_ref[c, first + low : first + high, :] for c in range(channel // LANES, (channel + STEP) // LANES)],
                axis=1,
            )
            for low, high in pieces
        ]
        return jnp.concatenate(found, axis=0).astype(jnp.bfloat16)

    def conv_steps(unit, pieces):
        def one(k, channel, total):
            first = unit * extended + (k - KERNEL // 2) * DILATIONS[unit]
            at = k * channels + channel
            part = jnp.dot(
                rows_of(first, pieces, channel), taps_ref[unit, at : at + STEP, :],
                preferred_element_type=jnp.float32,
            )
            return part if total is None else total + part
        return [
            functools.partial(one, k, channel)
            for k in range(KERNEL) for channel in range(0, channels, STEP)
        ]

    def mid_tasks(unit, pieces, h):
        def one(start, stop):
            g = snake(
                h[start:stop] + row_of(bias_wide, unit),
                row_of(alpha_mid, unit) * (1.0 / math.pi), 1.0 / row_of(beta_mid, unit),
            )
            for c in range(groups):
                held_ref[c, pl.ds(none + (gated_at + start), stop - start), :] = g[:, c * LANES : (c + 1) * LANES]
        return [functools.partial(one, *span) for span in blocks(0, h.shape[0])]

    def point(unit, size):
        total = None
        for channel in range(0, channels, STEP):
            part = jnp.dot(
                rows_of(gated_at, ((0, size),), channel), point_ref[unit, channel : channel + STEP, :],
                preferred_element_type=jnp.float32,
            )
            total = part if total is None else total + part
        return total

    def end_tasks(unit, pieces, update):
        def one(at, start, stop):
            kept = jnp.concatenate([x_ref[c, start:stop, :] for c in range(groups)], axis=1)
            x = (kept + (update[at : at + stop - start] + row_of(bias_point, unit))).astype(jnp.bfloat16)
            if unit + 1 < UNITS:
                hold(unit + 1, start, stop, x.astype(jnp.float32))
            else:
                out_ref[start - below : stop - below, :] = x
        tasks, base = [], 0
        for low, high in pieces:
            tasks += [functools.partial(one, base + start - low, start, stop) for start, stop in blocks(low, high)]
            base += high - low
        return tasks

    def size_of(pieces):
        return sum(high - low for low, high in pieces)

    core = ((below + STRIDE + TILE // 2, above - TILE),)
    rims = ((below - MARGIN[0], core[0][0]), (core[0][1], above + MARGIN[0]))
    wholes = [((below - MARGIN[unit], above + MARGIN[unit]),) for unit in range(UNITS)]

    def conv(unit, pieces, waits=None):
        total = None
        steps = conv_steps(unit, pieces)
        each = len(steps) // KERNEL
        for k in range(KERNEL):
            if waits is not None:
                waits[k].wait()
            for step in steps[k * each : (k + 1) * each]:
                total = step(total)
        return total

    def close(unit, pieces, h):
        for task in mid_tasks(unit, pieces, h):
            task()
        for task in end_tasks(unit, pieces, point(unit, size_of(pieces))):
            task()

    @pl.when(has_left & has_right)
    def _():
        pl.semaphore_wait(barrier, 2)

    @pl.when(has_left != has_right)
    def _():
        pl.semaphore_wait(barrier, 1)

    @pl.when(has_right)
    def _():
        to_right.start()

    @pl.when(has_left)
    def _():
        to_left.start()

    for copy in weights[1]:
        copy.start()
    for copy in weights[2]:
        copy.start()
    own.wait()
    for copy in smalls:
        copy.wait()
    for task in enter(below + STRIDE, above):
        task()
    for copy in weights[0]:
        copy.wait()
    h = conv(0, core)
    close(0, core, h)

    @pl.when(has_left)
    def _():
        to_right.wait_recv()

    @pl.when(has_right)
    def _():
        to_left.wait_recv()

    for unit in range(1, UNITS):
        for copy in weights[unit]:
            copy.wait()
    enter_halo()
    close(0, rims, conv(0, rims))
    for unit in range(1, UNITS):
        (low, high), = wholes[unit]
        half = low + (high - low) // (2 * TILE) * TILE
        parts = (((low, half),), ((half, high),))
        found = [conv(unit, part) for part in parts]
        for part, h in zip(parts, found):
            close(unit, part, h)

    @pl.when(has_right)
    def _():
        to_right.wait_send()

    @pl.when(has_left)
    def _():
        to_left.wait_send()


def per_device(
    upsampled, taps, bias_wide, pointwise, bias_point, alpha_in, beta_in, alpha_mid, beta_mid
):
    count = lax.axis_size("tm")
    frames, channels = upsampled.shape[1:]
    extended = frames + 2 * EDGE
    gated_at = UNITS * extended
    hbm = pl.BlockSpec(memory_space=pltpu.HBM)
    return pl.pallas_call(
        functools.partial(kernel, count, frames, gated_at),
        out_shape=pltpu.VMEM((frames, channels), jnp.bfloat16),
        in_specs=[hbm] * 9,
        out_specs=pl.BlockSpec(memory_space=pltpu.VMEM),
        scratch_shapes=[
            pltpu.VMEM((UNITS, KERNEL * channels, channels), jnp.bfloat16),
            pltpu.VMEM((UNITS, channels, channels), jnp.bfloat16),
            pltpu.VMEM((2, frames, channels), jnp.bfloat16),
            pltpu.VMEM((2, 2, EDGE, channels), jnp.bfloat16),
            pltpu.VMEM((channels // LANES, extended, LANES), jnp.float32),
            pltpu.VMEM((channels // LANES, gated_at + extended, LANES), jnp.float32),
        ]
        + [pltpu.VMEM((UNITS, channels), jnp.float32)] * 6
        + [
            pltpu.SemaphoreType.DMA((UNITS, KERNEL)),
            pltpu.SemaphoreType.DMA((UNITS,)),
            pltpu.SemaphoreType.DMA((6,)),
            pltpu.SemaphoreType.DMA,
            pltpu.SemaphoreType.DMA((2,)),
            pltpu.SemaphoreType.DMA((2,)),
        ],
        compiler_params=pltpu.CompilerParams(
            vmem_limit_bytes=58_000_000, collective_id=0, has_side_effects=True
        ),
    )(
        upsampled, taps.reshape(UNITS, KERNEL * channels, channels), bias_wide, pointwise,
        bias_point, alpha_in, beta_in, alpha_mid, beta_mid,
    )


def solution(mesh):
    placed = (P(None, ("grp", "tm"), None), P(), P(), P(), P(), P(), P(), P(), P())
    return jax.shard_map(
        per_device, mesh=mesh, in_specs=placed, out_specs=P(("grp", "tm"), None), check_vma=False
    )
```

```python
import functools
import math

import jax
import jax.numpy as jnp
from jax import lax
from jax.experimental import pallas as pl
from jax.experimental.pallas import tpu as pltpu
from jax.sharding import PartitionSpec as P

MESH = pl.DeviceIdType.MESH
KERNEL = 7
STRIDE = 8
UNITS = 3
DILATIONS = (1, 3, 9)
LANES = 128
TILE = 16
EDGE = 48
MARGIN = (40, 32, 0)
INSET = (64, 80, 112)
LEFT = (13, 11, 7)
STEP = 256
A, B, C, D = -1.8904849290847778, 1.368099570274353, -0.38957276940345764, -0.40598922967910767
SCALE = 10.581298828125


def snake(values, frequency, inverse):
    turns = values * frequency
    rest = turns - jnp.round(turns)
    square = rest * rest
    inner = (square + A) * square + B
    poly = ((inner + square) + C) * inner + D
    return values + poly * (square * (inverse * SCALE))


def blocks(low, high):
    edges = [low, *range(low - low % TILE + TILE, high, TILE), high]
    return list(zip(edges[:-1], edges[1:]))


def kernel(
    count, frames, gated_at,
    up_hbm, taps_hbm, bias_wide_hbm, point_hbm, bias_point_hbm,
    alpha_in_hbm, beta_in_hbm, alpha_mid_hbm, beta_mid_hbm,
    out_ref,
    taps_ref, point_ref, up_ref, halo_ref, x_ref, held_ref,
    bias_wide, bias_point, alpha_in, beta_in, alpha_mid, beta_mid,
    taps_sems, point_sems, small_sems, up_sem, send_sems, recv_sems,
):
    channels = up_ref.shape[2]
    groups = channels // LANES
    below, above = EDGE, EDGE + frames
    extended = frames + 2 * EDGE
    me = lax.axis_index("tm")
    has_left = me > 0
    has_right = me < count - 1
    barrier = pltpu.get_barrier_semaphore()

    @pl.when(has_left)
    def _():
        pl.semaphore_signal(barrier, inc=1, device_id={"tm": me - 1}, device_id_type=MESH)

    @pl.when(has_right)
    def _():
        pl.semaphore_signal(barrier, inc=1, device_id={"tm": me + 1}, device_id_type=MESH)

    own = pltpu.make_async_copy(up_hbm, up_ref, up_sem)
    own.start()
    smalls = [
        pltpu.make_async_copy(source, target, small_sems.at[i])
        for i, (source, target) in enumerate((
            (alpha_in_hbm, alpha_in), (beta_in_hbm, beta_in), (bias_wide_hbm, bias_wide),
            (alpha_mid_hbm, alpha_mid), (beta_mid_hbm, beta_mid), (bias_point_hbm, bias_point),
        ))
    ]
    for copy in smalls:
        copy.start()

    def tap_copy(unit, k):
        span = pl.ds(k * channels, channels)
        return pltpu.make_async_copy(
            taps_hbm.at[unit, span, :], taps_ref.at[unit, span, :], taps_sems.at[unit, k]
        )

    weights = []
    for unit in range(UNITS):
        point = pltpu.make_async_copy(point_hbm.at[unit], point_ref.at[unit], point_sems.at[unit])
        weights.append([*(tap_copy(unit, k) for k in range(KERNEL)), point])
    for copy in weights[0]:
        copy.start()

    to_right = pltpu.make_async_remote_copy(
        src_ref=up_hbm.at[:, pl.ds(frames - EDGE, EDGE), :], dst_ref=halo_ref.at[0],
        send_sem=send_sems.at[0], recv_sem=recv_sems.at[0],
        device_id={"tm": me + 1}, device_id_type=MESH,
    )
    to_left = pltpu.make_async_remote_copy(
        src_ref=up_hbm.at[:, pl.ds(0, EDGE), :], dst_ref=halo_ref.at[1],
        send_sem=send_sems.at[1], recv_sem=recv_sems.at[1],
        device_id={"tm": me - 1}, device_id_type=MESH,
    )

    @pl.when(jnp.logical_not(has_left))
    def _():
        halo_ref[0] = jnp.zeros(halo_ref.shape[1:], jnp.bfloat16)

    @pl.when(jnp.logical_not(has_right))
    def _():
        halo_ref[1] = jnp.zeros(halo_ref.shape[1:], jnp.bfloat16)

    def wide_rows(ref, part, low, high):
        start, stop = low - low % TILE, high + (-high) % TILE
        return ref[part, start:stop, :].astype(jnp.float32)[low - start : high - start]

    def rounded(values):
        return values.astype(jnp.bfloat16).astype(jnp.float32)

    def summed(low, high):
        return rounded(wide_rows(up_ref, 0, low, high) + wide_rows(up_ref, 1, low - STRIDE, high - STRIDE))

    def row_of(ref, unit):
        return ref[unit : unit + 1, :]

    def hold(unit, low, high, values):
        s = snake(values, row_of(alpha_in, unit) * (1.0 / math.pi), 1.0 / row_of(beta_in, unit))
        if high <= below:
            s = jnp.where(has_left, s, 0.0)
        elif low >= above:
            s = jnp.where(has_right, s, 0.0)
        for c in range(groups):
            part = slice(c * LANES, (c + 1) * LANES)
            x_ref[c, low:high, :] = values[:, part]
            held_ref[c, pl.ds((unit * extended + low), high - low), :] = s[:, part]

    def enter(low, high):
        def one(start, stop):
            hold(0, start, stop, summed(start - below, stop - below))
        return [functools.partial(one, *span) for span in blocks(low, high)]

    def enter_halo():
        near, far = [
            [halo_ref[side, part].astype(jnp.float32) for part in range(2)] for side in range(2)
        ]
        early = wide_rows(up_ref, 0, 0, STRIDE)
        late = wide_rows(up_ref, 1, frames - STRIDE, frames)
        late_near = jnp.concatenate([near[1][0:STRIDE], near[1]], axis=0)[0:EDGE]
        lower = near[0] + late_near
        upper = far[0] + jnp.concatenate([late, far[1]], axis=0)[0:EDGE]
        for start, stop in blocks(below - MARGIN[0], below):
            hold(0, start, stop, rounded(lower[start:stop]))
        hold(0, below, below + STRIDE, rounded(early + near[1][EDGE - STRIDE : EDGE]))
        for start, stop in blocks(above, above + MARGIN[0]):
            hold(0, start, stop, rounded(upper[start - above : stop - above]))

    def rows_of(first, pieces, channel):
        found = [
            jnp.concatenate(
                [held_ref[c, first + low : first + high, :] for c in range(channel // LANES, (channel + STEP) // LANES)],
                axis=1,
            )
            for low, high in pieces
        ]
        return jnp.concatenate(found, axis=0).astype(jnp.bfloat16)

    def conv_steps(unit, pieces):
        def one(k, channel, total):
            first = unit * extended + (k - KERNEL // 2) * DILATIONS[unit]
            at = k * channels + channel
            part = jnp.dot(
                rows_of(first, pieces, channel), taps_ref[unit, at : at + STEP, :],
                preferred_element_type=jnp.float32,
            )
            return part if total is None else total + part
        return [
            functools.partial(one, k, channel)
            for k in range(KERNEL) for channel in range(0, channels, STEP)
        ]

    def mid_tasks(unit, pieces, h):
        def one(start, stop):
            g = snake(
                h[start:stop] + row_of(bias_wide, unit),
                row_of(alpha_mid, unit) * (1.0 / math.pi), 1.0 / row_of(beta_mid, unit),
            )
            for c in range(groups):
                held_ref[c, pl.ds((gated_at + start), stop - start), :] = g[:, c * LANES : (c + 1) * LANES]
        return [functools.partial(one, *span) for span in blocks(0, h.shape[0])]

    def point(unit, size):
        total = None
        for channel in range(0, channels, STEP):
            part = jnp.dot(
                rows_of(gated_at, ((0, size),), channel), point_ref[unit, channel : channel + STEP, :],
                preferred_element_type=jnp.float32,
            )
            total = part if total is None else total + part
        return total

    def end_tasks(unit, pieces, update):
        def one(at, start, stop):
            kept = jnp.concatenate([x_ref[c, start:stop, :] for c in range(groups)], axis=1)
            x = (kept + (update[at : at + stop - start] + row_of(bias_point, unit))).astype(jnp.bfloat16)
            if unit + 1 < UNITS:
                hold(unit + 1, start, stop, x.astype(jnp.float32))
            else:
                out_ref[start - below : stop - below, :] = x
        tasks, base = [], 0
        for low, high in pieces:
            tasks += [functools.partial(one, base + start - low, start, stop) for start, stop in blocks(low, high)]
            base += high - low
        return tasks

    def size_of(pieces):
        return sum(high - low for low, high in pieces)

    core = ((below + STRIDE + TILE // 2, above - TILE),)
    rims = ((below - MARGIN[0], core[0][0]), (core[0][1], above + MARGIN[0]))
    wholes = [((below - MARGIN[unit], above + MARGIN[unit]),) for unit in range(UNITS)]

    def conv(unit, pieces, waits=None):
        total = None
        steps = conv_steps(unit, pieces)
        each = len(steps) // KERNEL
        for k in range(KERNEL):
            if waits is not None:
                waits[k].wait()
            for step in steps[k * each : (k + 1) * each]:
                total = step(total)
        return total

    def close(unit, pieces, h):
        for task in mid_tasks(unit, pieces, h):
            task()
        for task in end_tasks(unit, pieces, point(unit, size_of(pieces))):
            task()

    @pl.when(has_left & has_right)
    def _():
        pl.semaphore_wait(barrier, 2)

    @pl.when(has_left != has_right)
    def _():
        pl.semaphore_wait(barrier, 1)

    @pl.when(has_right)
    def _():
        to_right.start()

    @pl.when(has_left)
    def _():
        to_left.start()

    for copy in weights[1]:
        copy.start()
    for copy in weights[2]:
        copy.start()
    own.wait()
    for copy in smalls:
        copy.wait()
    for task in enter(below + STRIDE, above):
        task()
    for copy in weights[0]:
        copy.wait()
    h = conv(0, core)
    close(0, core, h)

    @pl.when(has_left)
    def _():
        to_right.wait_recv()

    @pl.when(has_right)
    def _():
        to_left.wait_recv()

    for unit in range(1, UNITS):
        for copy in weights[unit]:
            copy.wait()
    enter_halo()
    close(0, rims, conv(0, rims))
    for unit in range(1, UNITS):
        (low, high), = wholes[unit]
        half = low + (high - low) // (2 * TILE) * TILE
        parts = (((low, half),), ((half, high),))
        found = [conv(unit, part) for part in parts]
        for part, h in zip(parts, found):
            close(unit, part, h)

    @pl.when(has_right)
    def _():
        to_right.wait_send()

    @pl.when(has_left)
    def _():
        to_left.wait_send()


def per_device(
    upsampled, taps, bias_wide, pointwise, bias_point, alpha_in, beta_in, alpha_mid, beta_mid
):
    count = lax.axis_size("tm")
    frames, channels = upsampled.shape[1:]
    extended = frames + 2 * EDGE
    gated_at = UNITS * extended
    hbm = pl.BlockSpec(memory_space=pltpu.HBM)
    return pl.pallas_call(
        functools.partial(kernel, count, frames, gated_at),
        out_shape=pltpu.VMEM((frames, channels), jnp.bfloat16),
        in_specs=[hbm] * 9,
        out_specs=pl.BlockSpec(memory_space=pltpu.VMEM),
        scratch_shapes=[
            pltpu.VMEM((UNITS, KERNEL * channels, channels), jnp.bfloat16),
            pltpu.VMEM((UNITS, channels, channels), jnp.bfloat16),
            pltpu.VMEM((2, frames, channels), jnp.bfloat16),
            pltpu.VMEM((2, 2, EDGE, channels), jnp.bfloat16),
            pltpu.VMEM((channels // LANES, extended, LANES), jnp.float32),
            pltpu.VMEM((channels // LANES, gated_at + extended, LANES), jnp.float32),
        ]
        + [pltpu.VMEM((UNITS, channels), jnp.float32)] * 6
        + [
            pltpu.SemaphoreType.DMA((UNITS, KERNEL)),
            pltpu.SemaphoreType.DMA((UNITS,)),
            pltpu.SemaphoreType.DMA((6,)),
            pltpu.SemaphoreType.DMA,
            pltpu.SemaphoreType.DMA((2,)),
            pltpu.SemaphoreType.DMA((2,)),
        ],
        compiler_params=pltpu.CompilerParams(
            vmem_limit_bytes=58_000_000, collective_id=0, has_side_effects=True
        ),
    )(
        upsampled, taps.reshape(UNITS, KERNEL * channels, channels), bias_wide, pointwise,
        bias_point, alpha_in, beta_in, alpha_mid, beta_mid,
    )


def solution(mesh):
    placed = (P(None, ("grp", "tm"), None), P(), P(), P(), P(), P(), P(), P(), P())
    return jax.shard_map(
        per_device, mesh=mesh, in_specs=placed, out_specs=P(("grp", "tm"), None), check_vma=False
    )
```

```python
import functools
import math

import jax
import jax.numpy as jnp
from jax import lax
from jax.experimental import pallas as pl
from jax.experimental.pallas import tpu as pltpu
from jax.sharding import PartitionSpec as P

MESH = pl.DeviceIdType.MESH
KERNEL = 7
STRIDE = 8
UNITS = 3
DILATIONS = (1, 3, 9)
LANES = 128
TILE = 16
EDGE = 48
MARGIN = (40, 32, 0)
INSET = (64, 80, 112)
LEFT = (13, 11, 7)
STEP = 256
A, B, C, D = -1.8904849290847778, 1.368099570274353, -0.38957276940345764, -0.40598922967910767
SCALE = 10.581298828125


def snake(values, frequency, inverse):
    turns = values * frequency
    rest = turns - jnp.round(turns)
    square = rest * rest
    inner = (square + A) * square + B
    poly = ((inner + square) + C) * inner + D
    return values + poly * (square * (inverse * SCALE))


def blocks(low, high):
    edges = [low, *range(low - low % TILE + TILE, high, TILE), high]
    return list(zip(edges[:-1], edges[1:]))


def kernel(
    count, frames, gated_at,
    up_hbm, taps_hbm, bias_wide_hbm, point_hbm, bias_point_hbm,
    alpha_in_hbm, beta_in_hbm, alpha_mid_hbm, beta_mid_hbm,
    out_ref,
    taps_ref, point_ref, up_ref, halo_ref, x_ref, held_ref,
    bias_wide, bias_point, alpha_in, beta_in, alpha_mid, beta_mid,
    taps_sems, point_sems, small_sems, up_sem, send_sems, recv_sems,
):
    channels = up_ref.shape[2]
    groups = channels // LANES
    below, above = EDGE, EDGE + frames
    extended = frames + 2 * EDGE
    me = lax.axis_index("tm")
    has_left = me > 0
    has_right = me < count - 1
    barrier = pltpu.get_barrier_semaphore()

    @pl.when(has_left)
    def _():
        pl.semaphore_signal(barrier, inc=1, device_id={"tm": me - 1}, device_id_type=MESH)

    @pl.when(has_right)
    def _():
        pl.semaphore_signal(barrier, inc=1, device_id={"tm": me + 1}, device_id_type=MESH)

    own = pltpu.make_async_copy(up_hbm, up_ref, up_sem)
    own.start()
    smalls = [
        pltpu.make_async_copy(source, target, small_sems.at[i])
        for i, (source, target) in enumerate((
            (alpha_in_hbm, alpha_in), (beta_in_hbm, beta_in), (bias_wide_hbm, bias_wide),
            (alpha_mid_hbm, alpha_mid), (beta_mid_hbm, beta_mid), (bias_point_hbm, bias_point),
        ))
    ]
    for copy in smalls:
        copy.start()

    def tap_copy(unit, k):
        span = pl.ds(k * channels, channels)
        return pltpu.make_async_copy(
            taps_hbm.at[unit, span, :], taps_ref.at[unit, span, :], taps_sems.at[unit, k]
        )

    weights = []
    for unit in range(UNITS):
        point = pltpu.make_async_copy(point_hbm.at[unit], point_ref.at[unit], point_sems.at[unit])
        weights.append([*(tap_copy(unit, k) for k in range(KERNEL)), point])
    for copy in weights[0]:
        copy.start()

    to_right = pltpu.make_async_remote_copy(
        src_ref=up_hbm.at[:, pl.ds(frames - EDGE, EDGE), :], dst_ref=halo_ref.at[0],
        send_sem=send_sems.at[0], recv_sem=recv_sems.at[0],
        device_id={"tm": me + 1}, device_id_type=MESH,
    )
    to_left = pltpu.make_async_remote_copy(
        src_ref=up_hbm.at[:, pl.ds(0, EDGE), :], dst_ref=halo_ref.at[1],
        send_sem=send_sems.at[1], recv_sem=recv_sems.at[1],
        device_id={"tm": me - 1}, device_id_type=MESH,
    )

    @pl.when(jnp.logical_not(has_left))
    def _():
        halo_ref[0] = jnp.zeros(halo_ref.shape[1:], jnp.bfloat16)

    @pl.when(jnp.logical_not(has_right))
    def _():
        halo_ref[1] = jnp.zeros(halo_ref.shape[1:], jnp.bfloat16)

    def wide_rows(ref, part, low, high):
        start, stop = low - low % TILE, high + (-high) % TILE
        return ref[part, start:stop, :].astype(jnp.float32)[low - start : high - start]

    def rounded(values):
        return values.astype(jnp.bfloat16).astype(jnp.float32)

    def summed(low, high):
        return rounded(wide_rows(up_ref, 0, low, high) + wide_rows(up_ref, 1, low - STRIDE, high - STRIDE))

    def row_of(ref, unit):
        return ref[unit : unit + 1, :]

    def hold(unit, low, high, values):
        s = snake(values, row_of(alpha_in, unit) * (1.0 / math.pi), 1.0 / row_of(beta_in, unit))
        if high <= below:
            s = jnp.where(has_left, s, 0.0)
        elif low >= above:
            s = jnp.where(has_right, s, 0.0)
        for c in range(groups):
            part = slice(c * LANES, (c + 1) * LANES)
            x_ref[c, low:high, :] = values[:, part]
            held_ref[c, pl.ds((unit * extended + low), high - low), :] = s[:, part]

    def enter(low, high):
        def one(start, stop):
            hold(0, start, stop, summed(start - below, stop - below))
        return [functools.partial(one, *span) for span in blocks(low, high)]

    def enter_halo():
        near, far = [
            [halo_ref[side, part].astype(jnp.float32) for part in range(2)] for side in range(2)
        ]
        early = wide_rows(up_ref, 0, 0, STRIDE)
        late = wide_rows(up_ref, 1, frames - STRIDE, frames)
        late_near = jnp.concatenate([near[1][0:STRIDE], near[1]], axis=0)[0:EDGE]
        lower = near[0] + late_near
        upper = far[0] + jnp.concatenate([late, far[1]], axis=0)[0:EDGE]
        for start, stop in blocks(below - MARGIN[0], below):
            hold(0, start, stop, rounded(lower[start:stop]))
        hold(0, below, below + STRIDE, rounded(early + near[1][EDGE - STRIDE : EDGE]))
        for start, stop in blocks(above, above + MARGIN[0]):
            hold(0, start, stop, rounded(upper[start - above : stop - above]))

    def rows_of(first, pieces, channel):
        found = [
            jnp.concatenate(
                [held_ref[c, first + low : first + high, :] for c in range(channel // LANES, (channel + STEP) // LANES)],
                axis=1,
            )
            for low, high in pieces
        ]
        return jnp.concatenate(found, axis=0).astype(jnp.bfloat16)

    def conv_steps(unit, pieces):
        def one(k, channel, total):
            first = unit * extended + (k - KERNEL // 2) * DILATIONS[unit]
            at = k * channels + channel
            part = jnp.dot(
                rows_of(first, pieces, channel), taps_ref[unit, at : at + STEP, :],
                preferred_element_type=jnp.float32,
            )
            return part if total is None else total + part
        return [
            functools.partial(one, k, channel)
            for k in range(KERNEL) for channel in range(0, channels, STEP)
        ]

    def mid_tasks(unit, pieces, h):
        def one(start, stop):
            g = snake(
                h[start:stop] + row_of(bias_wide, unit),
                row_of(alpha_mid, unit) * (1.0 / math.pi), 1.0 / row_of(beta_mid, unit),
            )
            for c in range(groups):
                held_ref[c, pl.ds((gated_at + start), stop - start), :] = g[:, c * LANES : (c + 1) * LANES]
        return [functools.partial(one, *span) for span in blocks(0, h.shape[0])]

    def point(unit, size):
        total = None
        for channel in range(0, channels, STEP):
            part = jnp.dot(
                rows_of(gated_at, ((0, size),), channel), point_ref[unit, channel : channel + STEP, :],
                preferred_element_type=jnp.float32,
            )
            total = part if total is None else total + part
        return total

    def end_tasks(unit, pieces, update):
        def one(at, start, stop):
            kept = jnp.concatenate([x_ref[c, start:stop, :] for c in range(groups)], axis=1)
            x = (kept + (update[at : at + stop - start] + row_of(bias_point, unit))).astype(jnp.bfloat16)
            if unit + 1 < UNITS:
                hold(unit + 1, start, stop, x.astype(jnp.float32))
            else:
                out_ref[start - below : stop - below, :] = x
        tasks, base = [], 0
        for low, high in pieces:
            tasks += [functools.partial(one, base + start - low, start, stop) for start, stop in blocks(low, high)]
            base += high - low
        return tasks

    def size_of(pieces):
        return sum(high - low for low, high in pieces)

    core = ((below + STRIDE + TILE // 2, above - TILE),)
    rims = ((below - MARGIN[0], core[0][0]), (core[0][1], above + MARGIN[0]))
    wholes = [((below - MARGIN[unit], above + MARGIN[unit]),) for unit in range(UNITS)]

    def conv(unit, pieces, waits=None):
        total = None
        steps = conv_steps(unit, pieces)
        each = len(steps) // KERNEL
        for k in range(KERNEL):
            if waits is not None:
                waits[k].wait()
            for step in steps[k * each : (k + 1) * each]:
                total = step(total)
        return total

    def close(unit, pieces, h):
        for task in mid_tasks(unit, pieces, h):
            task()
        for task in end_tasks(unit, pieces, point(unit, size_of(pieces))):
            task()

    @pl.when(has_left & has_right)
    def _():
        pl.semaphore_wait(barrier, 2)

    @pl.when(has_left != has_right)
    def _():
        pl.semaphore_wait(barrier, 1)

    @pl.when(has_right)
    def _():
        to_right.start()

    @pl.when(has_left)
    def _():
        to_left.start()

    for copy in weights[1]:
        copy.start()
    for copy in weights[2]:
        copy.start()
    own.wait()
    for copy in smalls:
        copy.wait()
    for task in enter(below + STRIDE, above):
        task()
    for copy in weights[0]:
        copy.wait()
    h = conv(0, core)
    close(0, core, h)

    @pl.when(has_left)
    def _():
        to_right.wait_recv()

    @pl.when(has_right)
    def _():
        to_left.wait_recv()

    for unit in range(1, UNITS):
        for copy in weights[unit]:
            copy.wait()
    enter_halo()
    close(0, rims, conv(0, rims))
    for unit in range(1, UNITS):
        (low, high), = wholes[unit]
        half = low + (high - low) * 7 // (12 * TILE) * TILE
        parts = (((low, half),), ((half, high),))
        found = [conv(unit, part) for part in parts]
        for part, h in zip(parts, found):
            close(unit, part, h)

    @pl.when(has_right)
    def _():
        to_right.wait_send()

    @pl.when(has_left)
    def _():
        to_left.wait_send()


def per_device(
    upsampled, taps, bias_wide, pointwise, bias_point, alpha_in, beta_in, alpha_mid, beta_mid
):
    count = lax.axis_size("tm")
    frames, channels = upsampled.shape[1:]
    extended = frames + 2 * EDGE
    gated_at = UNITS * extended
    hbm = pl.BlockSpec(memory_space=pltpu.HBM)
    return pl.pallas_call(
        functools.partial(kernel, count, frames, gated_at),
        out_shape=pltpu.VMEM((frames, channels), jnp.bfloat16),
        in_specs=[hbm] * 9,
        out_specs=pl.BlockSpec(memory_space=pltpu.VMEM),
        scratch_shapes=[
            pltpu.VMEM((UNITS, KERNEL * channels, channels), jnp.bfloat16),
            pltpu.VMEM((UNITS, channels, channels), jnp.bfloat16),
            pltpu.VMEM((2, frames, channels), jnp.bfloat16),
            pltpu.VMEM((2, 2, EDGE, channels), jnp.bfloat16),
            pltpu.VMEM((channels // LANES, extended, LANES), jnp.float32),
            pltpu.VMEM((channels // LANES, gated_at + extended, LANES), jnp.float32),
        ]
        + [pltpu.VMEM((UNITS, channels), jnp.float32)] * 6
        + [
            pltpu.SemaphoreType.DMA((UNITS, KERNEL)),
            pltpu.SemaphoreType.DMA((UNITS,)),
            pltpu.SemaphoreType.DMA((6,)),
            pltpu.SemaphoreType.DMA,
            pltpu.SemaphoreType.DMA((2,)),
            pltpu.SemaphoreType.DMA((2,)),
        ],
        compiler_params=pltpu.CompilerParams(
            vmem_limit_bytes=58_000_000, collective_id=0, has_side_effects=True
        ),
    )(
        upsampled, taps.reshape(UNITS, KERNEL * channels, channels), bias_wide, pointwise,
        bias_point, alpha_in, beta_in, alpha_mid, beta_mid,
    )


def solution(mesh):
    placed = (P(None, ("grp", "tm"), None), P(), P(), P(), P(), P(), P(), P(), P())
    return jax.shard_map(
        per_device, mesh=mesh, in_specs=placed, out_specs=P(("grp", "tm"), None), check_vma=False
    )
```
